32 devices in a mesh: lat: 4 (over y, x), lon: 8 (over z, core).
Axes of the slice: x: 2, y: 2, z: 4, core: 2. Of those that a mesh axis runs over, the one named last changes fastest.
Arguments:
- members: float32 [80, 2, 256, 1024], P('lon', None, 'lat'), may hold values from -6 to 6
- obs_row: int32 [2, 4, 8, 64], P(None, 'lat', 'lon'), may hold values from 0 to 63
- obs_col: int32 [2, 4, 8, 64], P(None, 'lat', 'lon'), may hold values from 0 to 127
- obs_value: float32 [2, 4, 8, 64], P(None, 'lat', 'lon'), may hold values from -6 to 6
- obs_error: float32 [2, 4, 8, 64], P(None, 'lat', 'lon'), may hold values from 0.25 to 4
- obs_weight: float32 [2, 4, 8, 2, 64], P(None, 'lat', 'lon'), may hold values from 0.2 to 1
- obs_count: int32 [2, 4, 8], P(None, 'lat', 'lon'), may hold values from 8 to 64, as said below
Outputs:
- analysis: float32 [80, 2, 256, 1024], P('lon', None, 'lat')
The draws below stay inside these ranges and needn't reach their ends.
Inputs may be any that keep to these rules, and one draw needn't show every extreme that they name: The first obs_count slots of a tile hold its observations, the others are ignored; in each batch one tile holds 64. `obs_row`: row inside the owning tile. `obs_col`: column inside the owning tile.
All inputs are finite; a program needn't handle non-finite values.
Results may differ from the reference program's by a relative error of at most 0.0001.
Values sent between devices are 32-bit elements; how exact they have to be, the bound alone decides.
A program may use at most 192 MiB of HBM per device.

```python
import math
import jax
import jax.numpy as jnp
from jax import lax

K = 80
LEV = 2
CLAT = 64
CLON = 128
SLOTS = 64
NBATCH = 2
RAD = 48
BANDS = 4
SECTORS = 8
NLAT = 256
NLON = 1024


def draw_obs_count(key, part):
    low = max(SLOTS // 8, 1)
    first, second = jax.random.split(jax.random.fold_in(key, 17))
    tiles = BANDS * SECTORS
    counts = jax.random.randint(first, (NBATCH, tiles), low, SLOTS - low + 1)
    full_at = jax.random.randint(second, (NBATCH, 1), 0, tiles)
    counts = jnp.where(jnp.arange(tiles)[None, :] == full_at, SLOTS, counts)
    return counts.reshape(NBATCH, BANDS, SECTORS).astype(jnp.int32)


def plant(entries, own_key, low, largest):
    spot = [jax.random.randint(jax.random.fold_in(own_key, axis), (), 0, length) for axis, length in enumerate(entries.shape)]
    longest = entries.shape.index(max(entries.shape))
    next_to = spot[:longest] + [(spot[longest] + 1) % entries.shape[longest]] + spot[longest + 1:]
    return entries.at[tuple(spot)].set(low).at[tuple(next_to)].set(largest)


def shard_levels(key, dims, cuts, low, largest):
    def one(position, parts):
        steps = jax.random.uniform(jax.random.fold_in(jax.random.fold_in(key, 6), position), (parts,), jnp.float32, low / len(cuts), largest / len(cuts))
        return jnp.repeat(jnp.exp(steps), dims[position] // parts).reshape((-1,) + (1,) * (len(dims) - position - 1))

    level = one(*cuts[0])
    for cut in cuts[1:]:
        level = level * one(*cut)
    return level


def bell_draw(key, dims, scale, most, cuts=(), dtype=jnp.bfloat16):
    result = jax.random.normal(key, dims, jnp.float32) * scale
    if len(cuts) > 0:
        result = shard_levels(key, dims, cuts, -0.22, 0.18) * result
    return jnp.clip(result, min=-most, max=most).astype(dtype)


def setup_inputs(seed: int = 0) -> dict:
    seeds = jax.random.split(jax.random.key(seed), 8)
    members = bell_draw(seeds[0], (K, LEV, NLAT, NLON), 1.0, 6.0, ((0, 8), (2, 4)), jnp.float32)
    obs_row = plant(jax.random.randint(seeds[1], (NBATCH, BANDS, SECTORS, SLOTS), 0, CLAT), jax.random.fold_in(seeds[1], 1), 0, CLAT - 1).astype(jnp.int32)
    obs_col = plant(jax.random.randint(seeds[2], (NBATCH, BANDS, SECTORS, SLOTS), 0, CLON), jax.random.fold_in(seeds[2], 1), 0, CLON - 1).astype(jnp.int32)
    obs_value = bell_draw(seeds[3], (NBATCH, BANDS, SECTORS, SLOTS), 1.5, 6.0, ((1, 4), (2, 8)), jnp.float32)
    obs_error = jnp.clip(jnp.exp(math.log(4.0) - 2.7725887 * jax.random.uniform(seeds[4], (NBATCH, BANDS, SECTORS, SLOTS), jnp.float32) ** shard_levels(seeds[4], (NBATCH, BANDS, SECTORS, SLOTS), ((1, 4), (2, 8)), -0.2, 0.2)), 0.25, 4.0)
    obs_weight = jnp.clip(0.2 + 0.8 * jax.random.uniform(seeds[5], (NBATCH, BANDS, SECTORS, LEV, SLOTS), jnp.float32) ** shard_levels(seeds[5], (NBATCH, BANDS, SECTORS, LEV, SLOTS), ((1, 4), (2, 8)), -0.2, 0.2), 0.2, 1.0)
    obs_count = draw_obs_count(jax.random.fold_in(seeds[7], 71), 0)
    return {"members": members, "obs_row": obs_row, "obs_col": obs_col, "obs_value": obs_value, "obs_error": obs_error, "obs_weight": obs_weight, "obs_count": obs_count}


def gaspari(dist):
    z = dist / (0.5 * RAD)
    near = (((-0.25 * z + 0.5) * z + 0.625) * z - 5.0 / 3.0) * z * z + 1.0
    zfar = jnp.maximum(z, 1.0)
    far = ((((zfar / 12.0 - 0.5) * zfar + 0.625) * zfar + 5.0 / 3.0) * zfar - 5.0) * zfar + 4.0 - 2.0 / (3.0 * zfar)
    return jnp.where(z <= 1.0, near, jnp.where(z < 2.0, far, 0.0))

def reference(members, obs_row, obs_col, obs_value, obs_error, obs_weight, obs_count):
    state = members
    width = 2 * RAD + 1
    offsets = jnp.arange(-RAD, RAD + 1).astype(jnp.float32)
    taper_tab = gaspari(jnp.sqrt(offsets[:, None] ** 2 + offsets[None, :] ** 2))
    lat_base = (jnp.arange(BANDS) * CLAT).astype(jnp.int32)[:, None, None]
    lon_base = (jnp.arange(SECTORS) * CLON).astype(jnp.int32)[None, :, None]
    slot_ids = jnp.arange(SLOTS).astype(jnp.int32)[None, None, :]
    zero = jnp.zeros((), jnp.int32)
    for batch in range(NBATCH):
        glat = (obs_row[batch] + lat_base).reshape(-1).astype(jnp.int32)
        glon = (obs_col[batch] + lon_base).reshape(-1).astype(jnp.int32)
        weight = jnp.transpose(obs_weight[batch], (0, 1, 3, 2)).reshape(-1, LEV)
        valid = (slot_ids < obs_count[batch][:, :, None]).reshape(-1).astype(jnp.float32)
        err = obs_error[batch].reshape(-1)
        value = obs_value[batch].reshape(-1)
        picked = state[:, :, glat, glon]
        prior = jnp.einsum('klo,ol->ko', picked, weight, precision=lax.Precision.HIGHEST)
        prior_mean = lax.optimization_barrier(jnp.mean(prior, axis=0))
        prior_pert = prior - prior_mean
        spread = lax.optimization_barrier(jnp.sum(prior_pert * prior_pert, axis=0)) / (K - 1.0)
        denom = spread + err
        mean_coef = valid * (value - prior_mean) / denom
        pert_coef = valid / (denom * (1.0 + jnp.sqrt(err / denom)))
        mean = lax.optimization_barrier(jnp.mean(state, axis=0))
        pert = state - mean
        padded = jnp.pad(pert, ((0, 0), (0, 0), (RAD, RAD), (0, 0)))
        padded = jnp.concatenate([padded[..., NLON - RAD:], padded, padded[..., :RAD]], axis=-1)
        start = jnp.zeros(padded.shape, jnp.float32)

        def add_one(total, item):
            row, col, deviation, cmean, cpert = item
            window = lax.dynamic_slice(padded, (zero, zero, row, col), (K, LEV, width, width))
            cov = jnp.einsum('klyx,k->lyx', window, deviation, precision=lax.Precision.HIGHEST) / (K - 1.0)
            gain = cov * taper_tab
            coef = cmean - cpert * deviation
            delta = gain[None] * coef[:, None, None, None]
            current = lax.dynamic_slice(total, (zero, zero, row, col), (K, LEV, width, width))
            return (lax.dynamic_update_slice(total, current + delta, (zero, zero, row, col)), None)
        total, _ = lax.scan(add_one, start, (glat, glon, prior_pert.T, mean_coef, pert_coef))
        core = total[:, :, RAD:RAD + NLAT, :]
        inner = core[..., RAD:RAD + NLON]
        inner = inner.at[..., :RAD].add(core[..., RAD + NLON:])
        inner = inner.at[..., NLON - RAD:].add(core[..., :RAD])
        state = state + inner
    return state
```

```python
import functools

import jax
import jax.numpy as jnp
from jax import lax
from jax.experimental import pallas as pl
from jax.experimental.pallas import tpu as pltpu
from jax.sharding import PartitionSpec as P

NBATCH = 2
RAD = 48
CHUNKS = 4
HIGHEST = lax.Precision.HIGHEST


def extended(block, sides, width):
    for axis, dim in sides:
        count = lax.axis_size(axis)
        forward = [(i, (i + 1) % count) for i in range(count)]
        backward = [(target, source) for source, target in forward]
        low = lax.ppermute(
            lax.slice_in_dim(block, block.shape[dim] - width, None, axis=dim), axis, forward
        )
        high = lax.ppermute(lax.slice_in_dim(block, 0, width, axis=dim), axis, backward)
        block = jnp.concatenate([low, block, high], axis=dim)
    return block


def gaspari_sq(dist_sq):
    inverse = lax.rsqrt(jnp.maximum(dist_sq, 1e-12))
    z = dist_sq * inverse * (2.0 / RAD)
    near = (((-0.25 * z + 0.5) * z + 0.625) * z - 5.0 / 3.0) * (z * z) + 1.0
    far = (
        ((((z * (1.0 / 12.0) - 0.5) * z + 0.625) * z + 5.0 / 3.0) * z - 5.0) * z
        + 4.0
        - inverse * (RAD / 3.0)
    )
    return jnp.where(z <= 1.0, near, jnp.where(z < 2.0, far, 0.0))


def split(value):
    high = value.astype(jnp.bfloat16)
    low = (value - high.astype(jnp.float32)).astype(jnp.bfloat16)
    return high, low


def rounded(value):
    high = lax.reduce_precision(value, 8, 7)
    return high.astype(jnp.bfloat16), (value - high).astype(jnp.bfloat16)


def pick_kernel(rows_ref, cols_ref, members_ref, out_ref):
    sectors, slots = rows_ref.shape
    planes = out_ref.shape[1]
    clon = out_ref.shape[2]
    clat = members_ref.shape[0] // (planes * sectors)
    lane = lax.broadcasted_iota(jnp.int32, (planes, clon), 1)
    for sector in range(sectors):

        def step(slot, acc):
            row = rows_ref[sector, slot]
            col = cols_ref[sector, slot]
            slab = members_ref[pl.ds(sector * planes * clat + row, planes, stride=clat), :]
            moved = pltpu.roll(slab, lax.rem(slot - col + clon, clon), 1)
            return jnp.where(lane == slot, moved, acc)

        out_ref[sector] = lax.fori_loop(0, slots, step, jnp.zeros((planes, clon), jnp.float32), unroll=8)


def update_kernel(first, lo, hi, lat_ref, dx2_ref, prior_ref, coef_ref, state_ref, out_ref, *, full):
    rows = state_ref.shape[0] // (2 * full)

    def one_row(y, carry):
        cell_lat = (first + y).astype(jnp.float32)
        state = jnp.concatenate(
            [state_ref[pl.ds(l * rows + y, full, stride=2 * rows), :] for l in range(2)], axis=1
        )
        for batch in range(NBATCH):
            dy = lat_ref[batch, lo:hi, :] - cell_lat
            taper = gaspari_sq(dx2_ref[batch, lo:hi, :] + dy * dy)
            pert = state - jnp.mean(state, axis=0, keepdims=True)
            high, low = split(pert)
            stacked = jnp.concatenate([high, high, low], axis=0)
            cov = jnp.dot(prior_ref[batch, lo:hi, :], stacked, preferred_element_type=jnp.float32)
            ghigh, glow = split(cov * jnp.concatenate([taper, taper], axis=1))
            both = jnp.dot(coef_ref[batch, :, lo:hi], ghigh, preferred_element_type=jnp.float32)
            rest = jnp.dot(coef_ref[batch, :full, lo:hi], glow, preferred_element_type=jnp.float32)
            state = state + (both[:full] + (both[full:] + rest))
        clon = out_ref.shape[1]
        for l in range(2):
            out_ref[pl.ds(l * rows + y, full, stride=2 * rows), :] = state[:, l * clon : (l + 1) * clon]
        return carry

    lax.fori_loop(0, rows, one_row, 0)


def body(members, obs_row, obs_col, obs_value, obs_error, obs_weight, obs_count):
    parts = lax.axis_size("lon")
    group, levels, clat, nlon = members.shape
    full = group * parts
    clon = nlon // parts
    slots = obs_row.shape[-1]
    lat_first = lax.axis_index("lat") * clat
    lon_first = lax.axis_index("lon") * clon
    half = 0.5 * nlon

    places = jnp.concatenate([obs_row.reshape(1, -1), obs_col.reshape(1, -1)], axis=1)
    places = lax.all_gather(places, "lon", axis=0, tiled=True)
    sent = members.reshape(group, levels, clat, parts, clon).transpose(3, 0, 1, 2, 4)
    planes = group * levels
    picked = pl.pallas_call(
        pick_kernel,
        grid_spec=pltpu.PrefetchScalarGridSpec(
            num_scalar_prefetch=2,
            grid=(1,),
            in_specs=[pl.BlockSpec((parts * planes * clat, clon), lambda i, *_: (0, 0))],
            out_specs=pl.BlockSpec((parts, planes, clon), lambda i, *_: (0, 0, 0)),
        ),
        out_shape=jax.ShapeDtypeStruct((parts, planes, clon), jnp.float32),
        compiler_params=pltpu.CompilerParams(vmem_limit_bytes=48 << 20),
    )(places[:, : NBATCH * slots], places[:, NBATCH * slots :], sent.reshape(-1, clon))
    picked = lax.all_to_all(picked, "lon", split_axis=0, concat_axis=0, tiled=True)
    picked = picked.reshape(full, levels, clon)

    def packed_for(batch, points):
        prior = jnp.sum(points * obs_weight[batch, 0, 0][None], axis=1)
        valid = (jnp.arange(slots) < obs_count[batch, 0, 0]).astype(jnp.float32)
        prior_mean = jnp.mean(prior, axis=0)
        prior_pert = prior - prior_mean
        spread = jnp.sum(prior_pert * prior_pert, axis=0) / (full - 1.0)
        err = obs_error[batch, 0, 0]
        denom = spread + err
        mean_coef = valid * (obs_value[batch, 0, 0] - prior_mean) / denom
        pert_coef = valid / (denom * (1.0 + jnp.sqrt(err / denom)))
        glat = (lat_first + obs_row[batch, 0, 0]).astype(jnp.float32)
        glon = (lon_first + obs_col[batch, 0, 0]).astype(jnp.float32)
        extra = jnp.stack([mean_coef, pert_coef, glat, glon], axis=0)
        packed = jnp.concatenate([prior_pert, extra], axis=0)
        wide = extended(packed[:, None, None, :], (("lat", 1), ("lon", 2)), 1)
        received = wide.reshape(packed.shape[0], -1)
        prior_pert = received[:full]
        coef = received[full][None] - received[full + 1][None] * prior_pert
        return prior_pert * (1.0 / (full - 1.0)), coef, received[full + 2], received[full + 3]

    def lon_gap(first, second):
        return jnp.mod(first - second + half, 1.0 * nlon) - half

    one = packed_for(0, picked[:, :, :slots])
    points = picked[:, :, slots : 2 * slots]
    pert = points - jnp.mean(points, axis=0)
    dy = (lat_first + obs_row[1, 0, 0]).astype(jnp.float32)[None] - one[2][:, None]
    dx = lon_gap((lon_first + obs_col[1, 0, 0]).astype(jnp.float32)[None], one[3][:, None])
    taper = gaspari_sq(dx * dx + dy * dy)
    cov = jnp.einsum("ko,klp->olp", one[0], pert, precision=HIGHEST) * taper[:, None]
    points = points + jnp.einsum("ko,olp->klp", one[1], cov, precision=HIGHEST)
    two = packed_for(1, points)

    cell_lon = (lon_first + jnp.arange(clon)).astype(jnp.float32)
    lats, gaps, priors, coefs = [], [], [], []
    for prior_pert, coef, lat, lon in (one, two):
        lats.append(jnp.broadcast_to(lat[:, None], (lat.shape[0], clon)))
        dx = lon_gap(cell_lon[None], lon[:, None])
        gaps.append(dx * dx)
        high, low = rounded(prior_pert.T)
        priors.append(jnp.concatenate([high, low, high], axis=1))
        coefs.append(jnp.concatenate(rounded(coef), axis=0))
    lats, gaps, priors, coefs = (jnp.stack(v) for v in (lats, gaps, priors, coefs))

    rows = clat // CHUNKS
    third = lats.shape[1] // 3
    shifted = lats - lat_first.astype(jnp.float32)
    results = []
    for chunk in range(CHUNKS):
        first = chunk * rows
        low = 0 if first + 1 < RAD else third
        high = 3 * third if clat - (first + rows - 1) < RAD else 2 * third
        block = lax.all_to_all(
            sent[:, :, :, first : first + rows], "lon", split_axis=0, concat_axis=0, tiled=True
        )
        obs = 2 * NBATCH * (high - low) * full * levels * rows * clon
        done = pl.pallas_call(
            functools.partial(update_kernel, first, low, high, full=full),
            out_shape=jax.ShapeDtypeStruct((full * levels * rows, clon), jnp.float32),
            in_specs=[pl.BlockSpec(memory_space=pltpu.VMEM)] * 5,
            out_specs=pl.BlockSpec(memory_space=pltpu.VMEM),
            cost_estimate=pl.CostEstimate(flops=8 * obs, bytes_accessed=1 << 23, transcendentals=0),
            compiler_params=pltpu.CompilerParams(vmem_limit_bytes=32 << 20),
        )(shifted, gaps, priors, coefs, block.reshape(-1, clon))
        back = lax.all_to_all(
            done.reshape(parts, group, levels, rows, clon), "lon", split_axis=0, concat_axis=0, tiled=True
        )
        results.append(back.transpose(1, 2, 3, 0, 4).reshape(group, levels, rows, nlon))
    return jnp.concatenate(results, axis=2)


def solution(mesh):
    placed = (
        P("lon", None, "lat", None),
        P(None, "lat", "lon", None),
        P(None, "lat", "lon", None),
        P(None, "lat", "lon", None),
        P(None, "lat", "lon", None),
        P(None, "lat", "lon", None, None),
        P(None, "lat", "lon"),
    )
    return jax.shard_map(
        body, mesh=mesh, in_specs=placed, out_specs=P("lon", None, "lat", None), check_vma=False
    )
```

```python
import functools

import jax
import jax.numpy as jnp
from jax import lax
from jax.experimental import pallas as pl
from jax.experimental.pallas import tpu as pltpu
from jax.sharding import PartitionSpec as P

NBATCH = 2
RAD = 48
HIGHEST = lax.Precision.HIGHEST


def extended(block, sides, width):
    for axis, dim in sides:
        count = lax.axis_size(axis)
        forward = [(i, (i + 1) % count) for i in range(count)]
        backward = [(target, source) for source, target in forward]
        low = lax.ppermute(
            lax.slice_in_dim(block, block.shape[dim] - width, None, axis=dim), axis, forward
        )
        high = lax.ppermute(lax.slice_in_dim(block, 0, width, axis=dim), axis, backward)
        block = jnp.concatenate([low, block, high], axis=dim)
    return block


def gaspari_sq(dist_sq):
    inverse = lax.rsqrt(jnp.maximum(dist_sq, 1e-12))
    z = dist_sq * inverse * (2.0 / RAD)
    near = (((-0.25 * z + 0.5) * z + 0.625) * z - 5.0 / 3.0) * (z * z) + 1.0
    far = (
        ((((z * (1.0 / 12.0) - 0.5) * z + 0.625) * z + 5.0 / 3.0) * z - 5.0) * z
        + 4.0
        - inverse * (RAD / 3.0)
    )
    return jnp.where(z <= 1.0, near, jnp.where(z < 2.0, far, 0.0))


def split(value):
    high = value.astype(jnp.bfloat16)
    low = (value - high.astype(jnp.float32)).astype(jnp.bfloat16)
    return high, low


def rounded(value):
    high = lax.reduce_precision(value, 8, 7)
    return high.astype(jnp.bfloat16), (value - high).astype(jnp.bfloat16)


def pick_kernel(rows_ref, cols_ref, members_ref, out_ref):
    sectors, slots = rows_ref.shape
    planes = out_ref.shape[1]
    clon = out_ref.shape[2]
    clat = members_ref.shape[0] // (planes * sectors)
    lane = lax.broadcasted_iota(jnp.int32, (planes, clon), 1)
    for sector in range(sectors):

        def step(slot, acc):
            row = rows_ref[sector, slot]
            col = cols_ref[sector, slot]
            slab = members_ref[pl.ds(sector * planes * clat + row, planes, stride=clat), :]
            moved = pltpu.roll(slab, lax.rem(slot - col + clon, clon), 1)
            return jnp.where(lane == slot, moved, acc)

        out_ref[sector] = lax.fori_loop(0, slots, step, jnp.zeros((planes, clon), jnp.float32), unroll=8)


def update_kernel(pieces, lat_ref, dx2_ref, prior_ref, coef_ref, state_ref, out_ref):
    planes, rows, clon = out_ref.shape
    full = planes // 2
    state_flat = state_ref.reshape(planes * rows, clon)
    out_flat = out_ref.reshape(planes * rows, clon)
    first = pieces[0][0]

    for begin, end, lo, hi in pieces:

        def one_row(y, carry):
            cell_lat = y.astype(jnp.float32)
            spots = [pl.ds(l * rows + y - first, full, stride=2 * rows) for l in range(2)]
            state = jnp.concatenate([state_flat[spot, :] for spot in spots], axis=1)
            for batch in range(NBATCH):
                dy = lat_ref[batch, lo:hi, :] - cell_lat
                taper = gaspari_sq(dx2_ref[batch, lo:hi, :] + dy * dy)
                pert = state - jnp.mean(state, axis=0, keepdims=True)
                high, low = split(pert)
                stacked = jnp.concatenate([high, high, low], axis=0)
                cov = jnp.dot(prior_ref[batch, lo:hi, :], stacked, preferred_element_type=jnp.float32)
                ghigh, glow = split(cov * jnp.concatenate([taper, taper], axis=1))
                both = jnp.dot(coef_ref[batch, :, lo:hi], ghigh, preferred_element_type=jnp.float32)
                rest = jnp.dot(coef_ref[batch, :full, lo:hi], glow, preferred_element_type=jnp.float32)
                state = state + (both[:full] + (both[full:] + rest))
            for l, spot in enumerate(spots):
                out_flat[spot, :] = state[:, l * clon : (l + 1) * clon]
            return carry

        lax.fori_loop(begin, end, one_row, 0)


def body(members, obs_row, obs_col, obs_value, obs_error, obs_weight, obs_count):
    parts = lax.axis_size("lon")
    group, levels, clat, nlon = members.shape
    full = group * parts
    clon = nlon // parts
    slots = obs_row.shape[-1]
    lat_first = lax.axis_index("lat") * clat
    lon_first = lax.axis_index("lon") * clon
    half = 0.5 * nlon

    places = jnp.concatenate([obs_row.reshape(1, -1), obs_col.reshape(1, -1)], axis=1)
    sent = members.reshape(group, levels, clat, parts, clon).transpose(3, 0, 1, 2, 4)
    block = lax.all_to_all(sent, "lon", split_axis=0, concat_axis=0, tiled=True)
    block = block.reshape(full * levels, clat, clon)
    places, sent = lax.optimization_barrier((places, sent))
    places = lax.all_gather(places, "lon", axis=0, tiled=True)
    planes = group * levels
    picked = pl.pallas_call(
        pick_kernel,
        grid_spec=pltpu.PrefetchScalarGridSpec(
            num_scalar_prefetch=2,
            grid=(1,),
            in_specs=[pl.BlockSpec((parts * planes * clat, clon), lambda i, *_: (0, 0))],
            out_specs=pl.BlockSpec((parts, planes, clon), lambda i, *_: (0, 0, 0)),
        ),
        out_shape=jax.ShapeDtypeStruct((parts, planes, clon), jnp.float32),
        compiler_params=pltpu.CompilerParams(vmem_limit_bytes=48 << 20),
    )(places[:, : NBATCH * slots], places[:, NBATCH * slots :], sent.reshape(-1, clon))
    picked = lax.all_gather(picked, "lon", axis=0, tiled=False)
    picked = lax.dynamic_index_in_dim(picked, lax.axis_index("lon"), axis=1, keepdims=False)
    picked = picked.reshape(full, levels, clon)

    def packed_for(batch, points):
        prior = jnp.sum(points * obs_weight[batch, 0, 0][None], axis=1)
        valid = (jnp.arange(slots) < obs_count[batch, 0, 0]).astype(jnp.float32)
        prior_mean = jnp.mean(prior, axis=0)
        prior_pert = prior - prior_mean
        spread = jnp.sum(prior_pert * prior_pert, axis=0) / (full - 1.0)
        err = obs_error[batch, 0, 0]
        denom = spread + err
        mean_coef = valid * (obs_value[batch, 0, 0] - prior_mean) / denom
        pert_coef = valid / (denom * (1.0 + jnp.sqrt(err / denom)))
        glat = (lat_first + obs_row[batch, 0, 0]).astype(jnp.float32)
        glon = (lon_first + obs_col[batch, 0, 0]).astype(jnp.float32)
        extra = jnp.stack([mean_coef, pert_coef, glat, glon], axis=0)
        packed = jnp.concatenate([prior_pert, extra], axis=0)
        wide = extended(packed[:, None, None, :], (("lat", 1), ("lon", 2)), 1)
        received = wide.reshape(packed.shape[0], -1)
        prior_pert = received[:full]
        coef = received[full][None] - received[full + 1][None] * prior_pert
        return prior_pert * (1.0 / (full - 1.0)), coef, received[full + 2], received[full + 3]

    def lon_gap(first, second):
        return jnp.mod(first - second + half, 1.0 * nlon) - half

    one = packed_for(0, picked[:, :, :slots])
    points = picked[:, :, slots : 2 * slots]
    pert = points - jnp.mean(points, axis=0)
    dy = (lat_first + obs_row[1, 0, 0]).astype(jnp.float32)[None] - one[2][:, None]
    dx = lon_gap((lon_first + obs_col[1, 0, 0]).astype(jnp.float32)[None], one[3][:, None])
    taper = gaspari_sq(dx * dx + dy * dy)
    cov = jnp.einsum("ko,klp->olp", one[0], pert, precision=HIGHEST) * taper[:, None]
    points = points + jnp.einsum("ko,olp->klp", one[1], cov, precision=HIGHEST)
    two = packed_for(1, points)

    cell_lon = (lon_first + jnp.arange(clon)).astype(jnp.float32)
    lats, gaps, priors, coefs = [], [], [], []
    for prior_pert, coef, lat, lon in (one, two):
        lats.append(jnp.broadcast_to(lat[:, None], (lat.shape[0], clon)))
        dx = lon_gap(cell_lon[None], lon[:, None])
        gaps.append(dx * dx)
        high, low = rounded(prior_pert.T)
        priors.append(jnp.concatenate([high, low, high], axis=1))
        coefs.append(jnp.concatenate(rounded(coef), axis=0))
    lats, gaps, priors, coefs = (jnp.stack(v) for v in (lats, gaps, priors, coefs))

    third = lats.shape[1] // 3
    shifted = lats - lat_first.astype(jnp.float32)
    step = clat // 4

    def piece(begin, end):
        low = 0 if begin + 1 < RAD else third
        high = 3 * third if clat - (end - 1) < RAD else 2 * third
        return begin, end, low, high

    results = []
    for begin, end in ((0, step), (step, 2 * step), (2 * step, clat)):
        rows = end - begin
        pieces = tuple(piece(y, y + step) for y in range(begin, end, step))
        flops = sum(16 * NBATCH * (p[3] - p[2]) * full * levels * step * clon for p in pieces)
        done = pl.pallas_call(
            functools.partial(update_kernel, pieces),
            grid=(1,),
            out_shape=jax.ShapeDtypeStruct((full * levels, rows, clon), jnp.float32),
            in_specs=[pl.BlockSpec(v.shape, lambda i: (0, 0, 0)) for v in (shifted, gaps, priors, coefs)]
            + [pl.BlockSpec((full * levels, rows, clon), lambda i, at=begin // rows: (0, at, 0))],
            out_specs=pl.BlockSpec((full * levels, rows, clon), lambda i: (0, 0, 0)),
            cost_estimate=pl.CostEstimate(flops=8 * flops, bytes_accessed=1 << 23, transcendentals=0),
            compiler_params=pltpu.CompilerParams(vmem_limit_bytes=40 << 20),
        )(shifted, gaps, priors, coefs, block)
        back = lax.all_to_all(
            done.reshape(parts, group, levels, rows, clon), "lon", split_axis=0, concat_axis=0, tiled=True
        )
        results.append(back.transpose(1, 2, 3, 0, 4).reshape(group, levels, rows, nlon))
    return jnp.concatenate(results, axis=2)


def solution(mesh):
    placed = (
        P("lon", None, "lat", None),
        P(None, "lat", "lon", None),
        P(None, "lat", "lon", None),
        P(None, "lat", "lon", None),
        P(None, "lat", "lon", None),
        P(None, "lat", "lon", None, None),
        P(None, "lat", "lon"),
    )
    return jax.shard_map(
        body, mesh=mesh, in_specs=placed, out_specs=P("lon", None, "lat", None), check_vma=False
    )
```

```python
import functools

import jax
import jax.numpy as jnp
from jax import lax
from jax.experimental import pallas as pl
from jax.experimental.pallas import tpu as pltpu
from jax.sharding import PartitionSpec as P

NBATCH = 2
RAD = 48
HIGHEST = lax.Precision.HIGHEST


def extended(block, sides, width):
    for axis, dim in sides:
        count = lax.axis_size(axis)
        forward = [(i, (i + 1) % count) for i in range(count)]
        backward = [(target, source) for source, target in forward]
        low = lax.ppermute(
            lax.slice_in_dim(block, block.shape[dim] - width, None, axis=dim), axis, forward
        )
        high = lax.ppermute(lax.slice_in_dim(block, 0, width, axis=dim), axis, backward)
        block = jnp.concatenate([low, block, high], axis=dim)
    return block


def gaspari_sq(dist_sq):
    inverse = lax.rsqrt(jnp.maximum(dist_sq, 1e-12))
    z = dist_sq * inverse * (2.0 / RAD)
    near = (((-0.25 * z + 0.5) * z + 0.625) * z - 5.0 / 3.0) * (z * z) + 1.0
    far = (
        ((((z * (1.0 / 12.0) - 0.5) * z + 0.625) * z + 5.0 / 3.0) * z - 5.0) * z
        + 4.0
        - inverse * (RAD / 3.0)
    )
    return jnp.where(z <= 1.0, near, jnp.where(z < 2.0, far, 0.0))


def split(value):
    high = value.astype(jnp.bfloat16)
    low = (value - high.astype(jnp.float32)).astype(jnp.bfloat16)
    return high, low


def rounded(value):
    high = lax.reduce_precision(value, 8, 7)
    return high.astype(jnp.bfloat16), (value - high).astype(jnp.bfloat16)


def pick_kernel(rows_ref, cols_ref, members_ref, out_ref):
    sectors, slots = rows_ref.shape
    planes = out_ref.shape[1]
    clon = out_ref.shape[2]
    clat = members_ref.shape[0] // (planes * sectors)
    lane = lax.broadcasted_iota(jnp.int32, (planes, clon), 1)
    for sector in range(sectors):

        def step(slot, acc):
            row = rows_ref[sector, slot]
            col = cols_ref[sector, slot]
            slab = members_ref[pl.ds(sector * planes * clat + row, planes, stride=clat), :]
            moved = pltpu.roll(slab, lax.rem(slot - col + clon, clon), 1)
            return jnp.where(lane == slot, moved, acc)

        out_ref[sector] = lax.fori_loop(0, slots, step, jnp.zeros((planes, clon), jnp.float32), unroll=8)


def update_kernel(pieces, lat_ref, dx2_ref, prior_ref, coef_ref, state_ref, out_ref):
    planes, rows, clon = out_ref.shape
    full = planes // 2
    state_flat = state_ref.reshape(planes * rows, clon)
    out_flat = out_ref.reshape(planes * rows, clon)
    first = pieces[0][0]

    for begin, end, lo, hi in pieces:

        def one_row(y, carry):
            cell_lat = y.astype(jnp.float32)
            spots = [pl.ds(l * rows + y - first, full, stride=2 * rows) for l in range(2)]
            state = jnp.concatenate([state_flat[spot, :] for spot in spots], axis=1)
            for batch in range(NBATCH):
                dy = lat_ref[batch, lo:hi, :] - cell_lat
                taper = gaspari_sq(dx2_ref[batch, lo:hi, :] + dy * dy)
                pert = state - jnp.mean(state, axis=0, keepdims=True)
                high, low = split(pert)
                stacked = jnp.concatenate([high, high, low], axis=0)
                cov = jnp.dot(prior_ref[batch, lo:hi, :], stacked, preferred_element_type=jnp.float32)
                ghigh, glow = split(cov * jnp.concatenate([taper, taper], axis=1))
                both = jnp.dot(coef_ref[batch, :, lo:hi], ghigh, preferred_element_type=jnp.float32)
                rest = jnp.dot(coef_ref[batch, :full, lo:hi], glow, preferred_element_type=jnp.float32)
                state = state + (both[:full] + (both[full:] + rest))
            for l, spot in enumerate(spots):
                out_flat[spot, :] = state[:, l * clon : (l + 1) * clon]
            return carry

        lax.fori_loop(begin, end, one_row, 0)


def body(members, obs_row, obs_col, obs_value, obs_error, obs_weight, obs_count):
    parts = lax.axis_size("lon")
    group, levels, clat, nlon = members.shape
    full = group * parts
    clon = nlon // parts
    slots = obs_row.shape[-1]
    lat_first = lax.axis_index("lat") * clat
    lon_first = lax.axis_index("lon") * clon
    half = 0.5 * nlon

    places = jnp.concatenate([obs_row.reshape(1, -1), obs_col.reshape(1, -1)], axis=1)
    places = lax.all_gather(places, "lon", axis=0, tiled=True)
    places, members = lax.optimization_barrier((places, members))
    sent = members.reshape(group, levels, clat, parts, clon).transpose(3, 0, 1, 2, 4)
    block = lax.all_to_all(sent, "lon", split_axis=0, concat_axis=0, tiled=True)
    block = block.reshape(full * levels, clat, clon)
    planes = group * levels
    picked = pl.pallas_call(
        pick_kernel,
        grid_spec=pltpu.PrefetchScalarGridSpec(
            num_scalar_prefetch=2,
            grid=(1,),
            in_specs=[pl.BlockSpec((parts * planes * clat, clon), lambda i, *_: (0, 0))],
            out_specs=pl.BlockSpec((parts, planes, clon), lambda i, *_: (0, 0, 0)),
        ),
        out_shape=jax.ShapeDtypeStruct((parts, planes, clon), jnp.float32),
        compiler_params=pltpu.CompilerParams(vmem_limit_bytes=48 << 20),
    )(places[:, : NBATCH * slots], places[:, NBATCH * slots :], sent.reshape(-1, clon))
    me = lax.axis_index("lon")
    rotated = lax.dynamic_slice_in_dim(jnp.concatenate([picked, picked]), me, parts)
    arrived = [
        lax.ppermute(rotated[shift], "lon", [(i, (i + shift) % parts) for i in range(parts)])
        for shift in range(parts - 1, 0, -1)
    ]
    arrived = jnp.stack(arrived + [rotated[0]])
    picked = lax.dynamic_slice_in_dim(jnp.concatenate([arrived, arrived]), parts - 1 - me, parts)
    picked = picked.reshape(full, levels, clon)

    def packed_for(batch, points):
        prior = jnp.sum(points * obs_weight[batch, 0, 0][None], axis=1)
        valid = (jnp.arange(slots) < obs_count[batch, 0, 0]).astype(jnp.float32)
        prior_mean = jnp.mean(prior, axis=0)
        prior_pert = prior - prior_mean
        spread = jnp.sum(prior_pert * prior_pert, axis=0) / (full - 1.0)
        err = obs_error[batch, 0, 0]
        denom = spread + err
        mean_coef = valid * (obs_value[batch, 0, 0] - prior_mean) / denom
        pert_coef = valid / (denom * (1.0 + jnp.sqrt(err / denom)))
        glat = (lat_first + obs_row[batch, 0, 0]).astype(jnp.float32)
        glon = (lon_first + obs_col[batch, 0, 0]).astype(jnp.float32)
        extra = jnp.stack([mean_coef, pert_coef, glat, glon], axis=0)
        packed = jnp.concatenate([prior_pert, extra], axis=0)
        wide = extended(packed[:, None, None, :], (("lat", 1), ("lon", 2)), 1)
        received = wide.reshape(packed.shape[0], -1)
        prior_pert = received[:full]
        coef = received[full][None] - received[full + 1][None] * prior_pert
        return prior_pert * (1.0 / (full - 1.0)), coef, received[full + 2], received[full + 3]

    def lon_gap(first, second):
        return jnp.mod(first - second + half, 1.0 * nlon) - half

    one = packed_for(0, picked[:, :, :slots])
    points = picked[:, :, slots : 2 * slots]
    pert = points - jnp.mean(points, axis=0)
    dy = (lat_first + obs_row[1, 0, 0]).astype(jnp.float32)[None] - one[2][:, None]
    dx = lon_gap((lon_first + obs_col[1, 0, 0]).astype(jnp.float32)[None], one[3][:, None])
    taper = gaspari_sq(dx * dx + dy * dy)
    cov = jnp.einsum("ko,klp->olp", one[0], pert, precision=HIGHEST) * taper[:, None]
    points = points + jnp.einsum("ko,olp->klp", one[1], cov, precision=HIGHEST)
    two = packed_for(1, points)

    cell_lon = (lon_first + jnp.arange(clon)).astype(jnp.float32)
    lats, gaps, priors, coefs = [], [], [], []
    for prior_pert, coef, lat, lon in (one, two):
        lats.append(jnp.broadcast_to(lat[:, None], (lat.shape[0], clon)))
        dx = lon_gap(cell_lon[None], lon[:, None])
        gaps.append(dx * dx)
        high, low = rounded(prior_pert.T)
        priors.append(jnp.concatenate([high, low, high], axis=1))
        coefs.append(jnp.concatenate(rounded(coef), axis=0))
    lats, gaps, priors, coefs = (jnp.stack(v) for v in (lats, gaps, priors, coefs))

    third = lats.shape[1] // 3
    shifted = lats - lat_first.astype(jnp.float32)
    step = clat // 8

    def piece(begin, end):
        low = 0 if begin + 1 < RAD else third
        high = 3 * third if clat - (end - 1) < RAD else 2 * third
        return begin, end, low, high

    results = {}
    for begin, end in ((6 * step, clat), (0, 3 * step), (3 * step, 6 * step)):
        rows = end - begin
        pieces = []
        for y in range(begin, end, step):
            new = piece(y, y + step)
            if pieces and pieces[-1][2:] == new[2:]:
                new = (pieces.pop()[0],) + new[1:]
            pieces.append(new)
        flops = sum(16 * NBATCH * (p[3] - p[2]) * full * levels * (p[1] - p[0]) * clon for p in pieces)
        done = pl.pallas_call(
            functools.partial(update_kernel, pieces),
            grid=(1,),
            out_shape=jax.ShapeDtypeStruct((full * levels, rows, clon), jnp.float32),
            in_specs=[pl.BlockSpec(v.shape, lambda i: (0, 0, 0)) for v in (shifted, gaps, priors, coefs)]
            + [pl.BlockSpec((full * levels, rows, clon), lambda i, at=begin // rows: (0, at, 0))],
            out_specs=pl.BlockSpec((full * levels, rows, clon), lambda i: (0, 0, 0)),
            cost_estimate=pl.CostEstimate(flops=8 * flops, bytes_accessed=1 << 23, transcendentals=0),
            compiler_params=pltpu.CompilerParams(vmem_limit_bytes=40 << 20),
        )(shifted, gaps, priors, coefs, block)
        back = lax.all_to_all(
            done.reshape(parts, group, levels, rows, clon), "lon", split_axis=0, concat_axis=0, tiled=True
        )
        results[begin] = back.transpose(1, 2, 3, 0, 4).reshape(group, levels, rows, nlon)
    return jnp.concatenate([results[begin] for begin in sorted(results)], axis=2)


def solution(mesh):
    placed = (
        P("lon", None, "lat", None),
        P(None, "lat", "lon", None),
        P(None, "lat", "lon", None),
        P(None, "lat", "lon", None),
        P(None, "lat", "lon", None),
        P(None, "lat", "lon", None, None),
        P(None, "lat", "lon"),
    )
    return jax.shard_map(
        body, mesh=mesh, in_specs=placed, out_specs=P("lon", None, "lat", None), check_vma=False
    )
```
